512 devices in a mesh: tm: 128 (over z, y, core), panel: 4 (over x).
Axes of the slice: x: 4, y: 8, z: 8, core: 2. Of those that a mesh axis runs over, the one named last changes fastest.
Arguments:
- transitions: float32 [256, 1024, 1024], P('tm', None, 'panel'), may hold values from 0 to 1, as said below
- start_weights: float32 [1024], replicated, may hold values from 0.1 to 10
Outputs:
- window_kernel: float32 [128, 1024, 1024], P('tm', None, 'panel')
- occupancy: float32 [128, 1024], P('tm', 'panel')
The draws below stay inside these ranges and needn't reach their ends.
Inputs may be any that keep to these rules, and one draw needn't show every extreme that they name: `transitions`: every entry is nonnegative; each diagonal entry is 0.3 or more; each row sums to between 0.3 and 1.7.
All inputs are finite; a program needn't handle non-finite values.
Results may differ from the reference program's by a relative error of at most 0.0003.
Values sent between devices are 32-bit elements; how exact they have to be, the bound alone decides.
No kernel may reach another device: no remote copies, remote signals or barrier semaphores. Data moves between devices by JAX's collectives and lax.ppermute only.
A program may use at most 64 MiB of HBM per device.

```python
import math
import jax
import jax.numpy as jnp
from jax import lax

S = 1024
BLOCK = 2
LEVELS = 2
STEPS = 256
N_TM = 128


def draw_transitions(key, part):
    key_stay = jax.random.fold_in(key, 11)
    key_move = jax.random.fold_in(key, 12)
    stay = jax.random.uniform(key_stay, (STEPS, S, 1), jnp.float32, 0.3, 0.9)
    spread = jax.random.uniform(key_move, (STEPS, S, S), jnp.float32, 0.0, 1.0)
    rows_index = jnp.arange(S)[:, None]
    cols_index = jnp.arange(S)[None, :]
    identity = (rows_index == cols_index).astype(jnp.float32)
    half_width = max(2, min(32, S // 16))
    offset = (cols_index - rows_index - S // 4) % S
    distance = jnp.minimum(offset, S - offset)
    band = (distance <= half_width).astype(jnp.float32)
    weights = 0.5 / S + band * (1.5 / (2 * half_width + 1))
    return (1.0 - stay) * spread * weights + stay * identity


def setup_inputs(seed: int = 0) -> dict:
    seeds = jax.random.split(jax.random.key(seed), 3)
    return {
        "transitions": draw_transitions(jax.random.fold_in(seeds[2], 71), 0),
        "start_weights": jnp.clip(jnp.exp(jax.random.uniform(seeds[1], (S,), jnp.float32, math.log(0.1), math.log(10.0))), 0.1, 10.0),
    }


def matmul_high(left, right):
    return jnp.matmul(left, right, precision=lax.Precision.HIGHEST)


def reference(transitions, start_weights):
    blocks = transitions.reshape(N_TM, BLOCK, S, S)
    running = blocks[:, 0]
    for step in range(1, BLOCK):
        running = matmul_high(running, blocks[:, step])
    for level in range(LEVELS):
        reach = 2 ** level
        joined = matmul_high(running[:-reach], running[reach:])
        running = jnp.concatenate([running[:reach], joined], axis=0)
    window_kernel = running * jnp.float32(S)
    occupancy = jnp.einsum("s,bst->bt", start_weights, running, precision=lax.Precision.HIGHEST)
    return window_kernel, occupancy
```

```python
import functools

import jax
import jax.numpy as jnp
from jax import lax
from jax.experimental import pallas as pl
from jax.experimental.pallas import tpu as pltpu
from jax.sharding import PartitionSpec as P


TILE = 256
CHAIN_TILE = 512


def spec(panel, rows, index):
    a, j = panel
    if j is None:
        return pl.BlockSpec((rows, a.shape[1]), lambda i: (index(i), 0))
    return pl.BlockSpec((None, rows, a.shape[2]), lambda i: (j, index(i), 0))


def place():
    b = lax.axis_index("tm")
    return b // 2, lax.rem(b, 2), lax.axis_index("panel")


def high_low(a):
    high = a.astype(jnp.bfloat16)
    return high, (a - high.astype(jnp.float32)).astype(jnp.bfloat16)


def dot3(high, low, v_high, v_low):
    dot = functools.partial(jnp.dot, preferred_element_type=jnp.float32)
    return dot(high, v_high) + (dot(high, v_low) + dot(low, v_high))


def tile_product(x, left_refs, v_high, v_low):
    total = None
    for r, ref in enumerate(left_refs):
        depth = ref.shape[1]
        rows = pl.ds(pl.multiple_of(lax.rem(x + r, len(left_refs)) * depth, depth), depth)
        part = dot3(*high_low(ref[...]), v_high[rows, :], v_low[rows, :])
        total = part if total is None else total + part
    return total


def put(v_high, v_low, where, value):
    v_high[where], v_low[where] = high_low(value)


def call_kernel(kernel, out_shape, grid, specs, out_specs, scratch, args, flops, traffic):
    return pl.pallas_call(
        kernel,
        out_shape=out_shape,
        grid=(grid,),
        in_specs=specs,
        out_specs=out_specs,
        scratch_shapes=scratch,
        compiler_params=pltpu.CompilerParams(vmem_limit_bytes=67_000_000),
        cost_estimate=pl.CostEstimate(flops=flops, bytes_accessed=traffic, transcendentals=0),
    )(*args)


def only(on, index):
    return lambda i: jnp.where(place()[1] == on, index(i), 0)


def product_kernel(n_left, n_right, width, on, *refs):
    lefts, rights, (out, v_high, v_low) = refs[:n_left], refs[n_left : n_left + n_right], refs[n_left + n_right :]
    i = pl.program_id(0)
    _, core, x = place()

    @pl.when(core == on)
    def _():
        @pl.when(i == 0)
        def _():
            for j, ref in enumerate(rights):
                put(v_high, v_low, (slice(None), slice(j * width, (j + 1) * width)), ref[...])

        total = tile_product(x, lefts, v_high, v_low)
        for j in range(n_right):
            out[j] = total[:, j * width : (j + 1) * width]


def product(left, right, on):
    rows, depth = left[0][0].shape[-2:]
    width = right[0][0].shape[-1]
    n, full = len(right), len(left) * depth
    return call_kernel(
        functools.partial(product_kernel, len(left), n, width, on),
        jax.ShapeDtypeStruct((n, rows, width), jnp.float32),
        rows // TILE,
        [spec(p, TILE, only(on, lambda i: i)) for p in left] + [spec(p, rows, lambda i: 0) for p in right],
        pl.BlockSpec((n, TILE, width), lambda i: (0, only(on, lambda i: i)(i), 0)),
        [pltpu.VMEM((full, n * width), jnp.bfloat16)] * 2,
        [p[0] for p in left + right],
        6 * rows * full * n * width,
        4 * (rows * full + 2 * n * rows * width),
    )


def chain_kernel(counts, tiles, on, passes, *refs):
    n_left = sum(counts)
    lefts, (right, out, v_high, v_low) = refs[:n_left], refs[n_left:]
    i = pl.program_id(0)
    k, core, x = place()
    own = pl.ds(pl.multiple_of(lax.rem(i, tiles) * CHAIN_TILE, CHAIN_TILE), CHAIN_TILE)
    active = core == on

    @pl.when(active & (i == 0))
    def _():
        put(v_high, v_low, 0, right[...])

    at = 0
    for n, count in enumerate(counts):
        here = lefts[at : at + count]
        at += count
        now, later, last = n % 2, (n + 1) % 2, n + 1 == len(counts)

        def keep(total, later=later, last=last):
            if last:
                out[...] = total
            else:
                put(v_high, v_low, (later, own), total)

        mine = active & (i >= n * tiles) & (i < (n + 1) * tiles)
        skipped = passes[n] & (k == 0)

        @pl.when(mine & jnp.logical_not(skipped))
        def _(here=here, now=now, keep=keep):
            keep(tile_product(x, here, v_high.at[now], v_low.at[now]))

        @pl.when(mine & skipped)
        def _(now=now, keep=keep):
            keep(v_high[now, own, :].astype(jnp.float32) + v_low[now, own, :].astype(jnp.float32))


def chain(lefts, right, on, passes):
    rows, _ = lefts[0][0][0].shape[-2:]
    width = right[0].shape[-1]
    tiles, n = rows // CHAIN_TILE, len(lefts)
    specs = []
    for m, left in enumerate(lefts):
        specs += [spec(p, CHAIN_TILE, only(on, lambda i, m=m: jnp.clip(i - m * tiles, 0, tiles - 1))) for p in left]
    return call_kernel(
        functools.partial(chain_kernel, [len(left) for left in lefts], tiles, on, passes),
        jax.ShapeDtypeStruct((rows, width), jnp.float32),
        n * tiles,
        specs + [spec(right, rows, lambda i: 0)],
        pl.BlockSpec((CHAIN_TILE, width), lambda i: (only(on, lambda i: jnp.maximum(i - (n - 1) * tiles, 0))(i), 0)),
        [pltpu.VMEM((2, rows, width), jnp.bfloat16)] * 2,
        [p[0] for left in lefts for p in left] + [right[0]],
        6 * n * rows * rows * width,
        4 * (n * rows * rows + 2 * rows * width),
    )


def finish_kernel(scale, late, whole, early, start, token, window, occupancy):
    i = pl.program_id(0)
    k, core, _ = place()

    def write(ref):
        w = ref[...]
        window[...] = w * scale
        part = dot3(*high_low(start[...]), *high_low(w))
        occupancy[...] = jnp.where(i == 0, part, occupancy[...] + part)

    pl.when(core == 1)(functools.partial(write, late))
    pl.when((core == 0) & (k == 0))(functools.partial(write, whole))
    pl.when((core == 0) & (k > 0))(functools.partial(write, early))


def finish(late, whole, early, start, token):
    rows, width = late.shape
    tiles = [spec(p, CHAIN_TILE, lambda i: i) for p in ((late, None), whole, (early, None))]
    return call_kernel(
        functools.partial(finish_kernel, float(rows)),
        [jax.ShapeDtypeStruct((rows, width), jnp.float32), jax.ShapeDtypeStruct((1, width), jnp.float32)],
        rows // CHAIN_TILE,
        tiles + [pl.BlockSpec((1, CHAIN_TILE), lambda i: (0, i)), pl.BlockSpec(memory_space=pl.ANY)],
        [pl.BlockSpec((CHAIN_TILE, width), lambda i: (i, 0)), pl.BlockSpec((1, width), lambda i: (0, 0))],
        [],
        [late, whole[0], early, start, token],
        4 * rows * width,
        16 * rows * width,
    )


def body(transitions, start_weights):
    n_tm, n_x = lax.axis_size("tm"), lax.axis_size("panel")
    n_chips = n_tm // 2

    def send(a, even=None, odd=None, wrap=False):
        pairs = []
        for kk in range(n_chips):
            for cc, to in enumerate((even, odd)):
                for xx in range(n_x):
                    if to is not None and (wrap or 0 <= kk + to[0] < n_chips):
                        there = (kk + to[0]) % n_chips * 2 + to[1]
                        pairs.append(((kk * 2 + cc) * n_x + xx, there * n_x + (xx + to[2]) % n_x))
        return lax.ppermute(a, ("tm", "panel"), pairs)

    a, c = transitions[0], lax.optimization_barrier(transitions)[1]
    a_left = send(a, (0, 0, 1), (1, 1, 0), wrap=True)
    c_right = send(c, (0, 0, -1))
    c_left = send(c, (0, 0, 1), (1, 1, 0), wrap=True)
    a_right = send(a, (0, 0, -1))
    a_far = send(a_left, (0, 0, 1))
    c_far = send(c_right, (0, 0, -1))
    token = send(c_left[:8, :128], (0, 1, 0))
    a_odd, c_odd = a_left, c_left
    a_odd_left = send(a_odd, None, (0, 1, 1))
    a_odd_right = send(a_odd, None, (0, 1, -1))
    c_odd_right = send(c_odd, None, (0, 1, -1))
    a_odd_far = send(a_odd_left, None, (0, 1, 1))
    c_odd_left = send(c_odd, None, (0, 1, 1))
    c_odd_far = send(c_odd_right, None, (0, 1, -1))

    def panels(own, right, far, left):
        return [own, (right, None), (far, None), (left, None)]

    def stacked(p):
        return [(p, j) for j in range(n_x)]

    left = panels((transitions, 0), a_right, a_far, a_left)
    right = panels((transitions, 1), c_right, c_far, c_left)
    even = product(left, right, 0)
    even_here = stacked(send(even, (0, 1, 0)))
    even_before = stacked(send(even, (1, 1, 0)))
    left = panels((a_odd, None), a_odd_right, a_odd_far, a_odd_left)
    right = panels((c_odd, None), c_odd_right, c_odd_far, c_odd_left)
    step = chain([right, left], even_here[0], 1, (True, True))
    there = send(step, None, (-1, 1, 0))
    ahead = chain([left], right[0], 1, (False,))
    ahead = send(ahead, None, (-1, 0, 0), wrap=True)
    odd = stacked(product(left, right, 1))
    cross = chain([stacked(even)], (ahead, None), 0, (False,))
    cross = send(cross, (0, 1, 0))
    step = chain([even_here, odd], (there, None), 1, (False, True))
    early = send(step, None, (1, 0, 0))
    late = chain([odd, even_before], (cross, None), 1, (True, True))
    window, occupancy = finish(late, (even, 0), early, start_weights[None, :], token)
    return window[None], occupancy


def solution(mesh):
    return jax.shard_map(
        body,
        mesh=mesh,
        in_specs=(P("tm", None, "panel"), P()),
        out_specs=(P("tm", None, "panel"), P("tm", "panel")),
        check_vma=False,
    )
```

```python
import functools

import jax
import jax.numpy as jnp
from jax import lax
from jax.experimental import pallas as pl
from jax.experimental.pallas import tpu as pltpu
from jax.sharding import PartitionSpec as P


TILE = 256
CHAIN_TILE = 512


def spec(panel, rows, index):
    a, j = panel
    if j is None:
        return pl.BlockSpec((rows, a.shape[1]), lambda i: (index(i), 0))
    return pl.BlockSpec((None, rows, a.shape[2]), lambda i: (j, index(i), 0))


def place():
    b = lax.axis_index("tm")
    return b // 2, lax.rem(b, 2), lax.axis_index("panel")


def high_low(a):
    high = a.astype(jnp.bfloat16)
    return high, (a - high.astype(jnp.float32)).astype(jnp.bfloat16)


def dot3(high, low, v_high, v_low):
    dot = functools.partial(jnp.dot, preferred_element_type=jnp.float32)
    return dot(high, v_high) + (dot(high, v_low) + dot(low, v_high))


def put(v, x, block, columns, value):
    depth = value.shape[0]
    n = v.shape[0] // (3 * depth)
    at = lax.rem(block - x + n, n) * depth
    high, low = high_low(value)
    for part, a in enumerate((high, low, high)):
        v[pl.ds(pl.multiple_of(at + part * n * depth, depth), depth), columns] = a


def put_all(v, x, columns, ref, depth):
    for block in range(ref.shape[0] // depth):
        put(v, x, block, columns, ref[block * depth : (block + 1) * depth, :])


def tile_product(left_refs, v):
    high, low = high_low(jnp.concatenate([ref[...] for ref in left_refs], axis=1))
    return jnp.dot(jnp.concatenate([high, high, low], axis=1), v[...], preferred_element_type=jnp.float32)


def call_kernel(kernel, out_shape, grid, specs, out_specs, scratch, args, flops, traffic):
    return pl.pallas_call(
        kernel,
        out_shape=out_shape,
        grid=(grid,),
        in_specs=specs,
        out_specs=out_specs,
        scratch_shapes=scratch,
        compiler_params=pltpu.CompilerParams(vmem_limit_bytes=67_000_000),
        cost_estimate=pl.CostEstimate(flops=flops, bytes_accessed=traffic, transcendentals=0),
    )(*[pltpu.with_memory_space_constraint(a, pltpu.HBM) for a in args])


def only(on, index):
    return lambda i: jnp.where(place()[1] == on, index(i), 0)


def product_kernel(n_left, picks, width, on, *refs):
    n_right = len(picks)
    lefts, rights, (out, held, v, sems) = refs[:n_left], refs[n_left : n_left + n_right], refs[n_left + n_right :]
    i = pl.program_id(0)
    _, core, x = place()

    @pl.when(core == on)
    def _():
        @pl.when(i == 0)
        def _():
            copies = []
            for j, ref in enumerate(rights):
                source = ref if picks[j] is None else ref.at[picks[j]]
                copies.append(pltpu.make_async_copy(source, held.at[j], sems.at[j]))
                copies[j].start()
            for j, copy in enumerate(copies):
                copy.wait()
                put_all(v, x, slice(j * width, (j + 1) * width), held.at[j], lefts[0].shape[1])

        total = tile_product(lefts, v)
        for j in range(n_right):
            out[j] = total[:, j * width : (j + 1) * width]


def product(left, right, on):
    rows, depth = left[0][0].shape[-2:]
    width = right[0][0].shape[-1]
    n, full = len(right), len(left) * depth
    step = only(on, lambda i: i)
    return call_kernel(
        functools.partial(product_kernel, len(left), [p[1] for p in right], width, on),
        jax.ShapeDtypeStruct((n, rows, width), jnp.float32),
        rows // TILE,
        [spec(p, TILE, step) for p in left] + [pl.BlockSpec(memory_space=pl.ANY)] * n,
        pl.BlockSpec((n, TILE, width), lambda i: (0, step(i), 0)),
        [
            pltpu.VMEM((n, rows, width), jnp.float32),
            pltpu.VMEM((3 * full, n * width), jnp.bfloat16),
            pltpu.SemaphoreType.DMA((n,)),
        ],
        [p[0] for p in left + right],
        6 * rows * full * n * width,
        4 * (rows * full + 2 * n * rows * width),
    )


def chain_kernel(counts, tiles, on, passes, *refs):
    n_left = sum(counts)
    lefts, (right, out, v) = refs[:n_left], refs[n_left:]
    i = pl.program_id(0)
    k, core, x = place()
    depth = lefts[0].shape[1]
    blocks = CHAIN_TILE // depth
    tile = lax.rem(i, tiles)
    active = core == on

    @pl.when(active & (i == 0))
    def _():
        put_all(v.at[0], x, slice(None), right, depth)

    at = 0
    for n, count in enumerate(counts):
        here = lefts[at : at + count]
        at += count
        now, later, last = n % 2, (n + 1) % 2, n + 1 == len(counts)
        mine = active & (i >= n * tiles) & (i < (n + 1) * tiles)
        skipped = passes[n] & (k == 0)

        @pl.when(mine & jnp.logical_not(skipped))
        def _(here=here, now=now, later=later, last=last):
            total = tile_product(here, v.at[now])
            if last:
                out[...] = total
            else:
                for h in range(blocks):
                    put(v.at[later], x, tile * blocks + h, slice(None), total[h * depth : (h + 1) * depth])

        @pl.when(mine & skipped)
        def _(now=now, later=later, last=last):
            for h in range(blocks):
                block = lax.rem(tile * blocks + h - x + count, count) * depth
                high = v[now, pl.ds(pl.multiple_of(block, depth), depth), :].astype(jnp.float32)
                low = v[now, pl.ds(pl.multiple_of(block + count * depth, depth), depth), :].astype(jnp.float32)
                if last:
                    out[h * depth : (h + 1) * depth, :] = high + low
                else:
                    put(v.at[later], x, tile * blocks + h, slice(None), high + low)


def chain(lefts, right, on, passes):
    rows, _ = lefts[0][0][0].shape[-2:]
    width = right[0].shape[-1]
    tiles, n = rows // CHAIN_TILE, len(lefts)
    specs = []
    for m, left in enumerate(lefts):
        specs += [spec(p, CHAIN_TILE, only(on, lambda i, m=m: jnp.clip(i - m * tiles, 0, tiles - 1))) for p in left]
    return call_kernel(
        functools.partial(chain_kernel, [len(left) for left in lefts], tiles, on, passes),
        jax.ShapeDtypeStruct((rows, width), jnp.float32),
        n * tiles,
        specs + [spec(right, rows, lambda i: 0)],
        pl.BlockSpec((CHAIN_TILE, width), lambda i: (only(on, lambda i: jnp.maximum(i - (n - 1) * tiles, 0))(i), 0)),
        [pltpu.VMEM((2, 3 * rows, width), jnp.bfloat16)],
        [p[0] for left in lefts for p in left] + [right[0]],
        6 * n * rows * rows * width,
        4 * (n * rows * rows + 2 * rows * width),
    )


def pair_kernel(places, n_x, done, *refs):
    lefts, rights, refs = refs[: len(places)], refs[len(places) : len(places) + 2], refs[len(places) + 2 :]
    i = pl.program_id(0)
    k, core, x = place()
    depth, width, n = lefts[0].shape[1], rights[0].shape[1], len(places)
    v = refs[-1]

    @pl.when(core == 1)
    def _():
        @pl.when(i == 0)
        def _():
            for j, ref in enumerate(rights):
                for at, r in enumerate(places):
                    block = lax.rem(x + r, n_x) * depth
                    high, low = high_low(ref[pl.ds(pl.multiple_of(block, depth), depth), :])
                    for part, a in enumerate((high, low, high)):
                        row = (part * n + at) * depth
                        v[row : row + depth, j * width : (j + 1) * width] = a

        total = tile_product(lefts, v)
        if done:
            begun, passed, step, ahead = refs[:4]
            step[...] = jnp.where(k == 0, passed[...], total[:, :width] + begun[0])
            ahead[...] = total[:, width:] + begun[1]
        else:
            refs[0][0] = total[:, :width]
            refs[0][1] = total[:, width:]


def pair(left, right, begun=None, passed=None):
    first = next(iter(left.values()))
    rows, depth = first[0].shape[-2:]
    width = right[0][0].shape[-1]
    n = len(left)
    both = pl.BlockSpec((2, CHAIN_TILE, width), lambda i: (0, i, 0))
    one = pl.BlockSpec((CHAIN_TILE, width), lambda i: (i, 0))
    f32 = jnp.float32
    specs = [spec(p, CHAIN_TILE, lambda i: i) for p in left.values()] + [spec(p, rows, lambda i: 0) for p in right]
    args = [p[0] for p in [*left.values(), *right]]
    if begun is None:
        out, out_specs = jax.ShapeDtypeStruct((2, rows, width), f32), both
    else:
        out, out_specs = [jax.ShapeDtypeStruct((rows, width), f32)] * 2, [one, one]
        specs += [both, spec(passed, CHAIN_TILE, lambda i: i)]
        args += [begun, passed[0]]
    return call_kernel(
        functools.partial(pair_kernel, tuple(left), rows // depth, begun is not None),
        out,
        rows // CHAIN_TILE,
        specs,
        out_specs,
        [pltpu.VMEM((3 * n * depth, 2 * width), jnp.bfloat16)],
        args,
        12 * rows * n * depth * width,
        4 * (rows * n * depth + 6 * rows * width),
    )


def finish_kernel(scale, late, whole, early, start, token, window, occupancy):
    i = pl.program_id(0)
    k, core, _ = place()

    def write(ref):
        w = ref[...]
        window[...] = w * scale
        part = dot3(*high_low(start[...]), *high_low(w))
        occupancy[...] = jnp.where(i == 0, part, occupancy[...] + part)

    pl.when(core == 1)(functools.partial(write, late))
    pl.when((core == 0) & (k == 0))(functools.partial(write, whole))
    pl.when((core == 0) & (k > 0))(functools.partial(write, early))


def finish(late, whole, early, start, token):
    rows, width = late.shape

    def used(role):
        def index(i):
            k, core, _ = place()
            return jnp.where(jnp.where(core == 1, 0, jnp.where(k == 0, 1, 2)) == role, i, 0)

        return index

    tiles = [spec(p, CHAIN_TILE, used(n)) for n, p in enumerate(((late, None), whole, (early, None)))]
    return call_kernel(
        functools.partial(finish_kernel, float(rows)),
        [jax.ShapeDtypeStruct((rows, width), jnp.float32), jax.ShapeDtypeStruct((1, width), jnp.float32)],
        rows // CHAIN_TILE,
        tiles + [pl.BlockSpec((1, CHAIN_TILE), lambda i: (0, i)), pl.BlockSpec(memory_space=pl.ANY)],
        [pl.BlockSpec((CHAIN_TILE, width), lambda i: (i, 0)), pl.BlockSpec((1, width), lambda i: (0, 0))],
        [],
        [late, whole[0], early, start, token],
        4 * rows * width,
        16 * rows * width,
    )


def body(transitions, start_weights):
    n_tm, n_x = lax.axis_size("tm"), lax.axis_size("panel")
    n_chips = n_tm // 2

    def send(a, even=None, odd=None, wrap=False, since=0):
        pairs = []
        for kk in range(since, n_chips):
            for cc, to in enumerate((even, odd)):
                for xx in range(n_x):
                    if to is not None and (wrap or 0 <= kk + to[0] < n_chips):
                        there = (kk + to[0]) % n_chips * 2 + to[1]
                        pairs.append(((kk * 2 + cc) * n_x + xx, there * n_x + (xx + to[2]) % n_x))
        return lax.ppermute(a, ("tm", "panel"), pairs)

    a, c = transitions[0], lax.optimization_barrier(transitions)[1]
    a_left = send(a, (0, 0, 1), (1, 1, 0), wrap=True)
    c_right = send(c, (0, 0, -1))
    c_left = send(c, (0, 0, 1), (1, 1, 0), wrap=True)
    a_right = send(a, (0, 0, -1))
    a_far = send(a_left, (0, 0, 1))
    c_far = send(c_right, (0, 0, -1))
    token = c_left[:8, :128]
    token = send(token, (0, 1, 0))
    a_odd, c_odd = a_left, c_left
    c_odd_left = send(c_odd, None, (0, 1, 1), since=1)
    a_odd_right = send(a_odd, None, (0, 1, -1))
    c_odd_right = send(c_odd, None, (0, 1, -1), since=1)
    c_odd_far = send(c_odd_left, None, (0, 1, 1), since=1)
    a_odd_far = send(a_odd_right, None, (0, 1, -1))
    a_odd_left = send(a_odd, None, (0, 1, 1))

    def panels(own, right, far, left):
        return [own, (right, None), (far, None), (left, None)]

    def stacked(p):
        return [(p, j) for j in range(n_x)]

    left = panels((transitions, 0), a_right, a_far, a_left)
    right = panels((transitions, 1), c_right, c_far, c_left)
    even = product(left, right, 0)
    even_here = stacked(send(even, (0, 1, 0)))
    even_before = stacked(send(even, (1, 1, 0)))
    left = panels((a_odd, None), a_odd_right, a_odd_far, a_odd_left)
    right = panels((c_odd, None), c_odd_right, c_odd_far, c_odd_left)
    here = even_here[0]
    inner = chain([right], here, 1, (False,))
    pairs = [(inner, None), right[0]]
    begun = pair({0: left[0], 1: left[1]}, pairs)
    step, ahead = pair({2: left[2], 3: left[3]}, pairs, begun, here)
    there = send(step, None, (-1, 1, 0))
    own = ahead
    ahead = send(ahead, None, (-1, 1, 0), wrap=True)
    rest = product(left, right[1:], 1)
    odd = [(own, None)] + [(rest, j) for j in range(n_x - 1)]
    step = chain([even_here, odd], (there, None), 1, (False, True))
    early = send(step, None, (1, 0, 0))
    late = chain([even_here, odd, even_before], (ahead, None), 1, (False, True, True))
    window, occupancy = finish(late, (even, 0), early, start_weights[None, :], token)
    return window[None], occupancy


def solution(mesh):
    return jax.shard_map(
        body,
        mesh=mesh,
        in_specs=(P("tm", None, "panel"), P()),
        out_specs=(P("tm", None, "panel"), P("tm", "panel")),
        check_vma=False,
    )
```

```python
import functools

import jax
import jax.numpy as jnp
from jax import lax
from jax.experimental import pallas as pl
from jax.experimental.pallas import tpu as pltpu
from jax.sharding import PartitionSpec as P


TILE = 256
CHAIN_TILE = 512


def spec(panel, rows, index):
    a, j = panel
    if j is None:
        return pl.BlockSpec((rows, a.shape[1]), lambda i: (index(i), 0))
    return pl.BlockSpec((None, rows, a.shape[2]), lambda i: (j, index(i), 0))


def place():
    b = lax.axis_index("tm")
    return b // 2, lax.rem(b, 2), lax.axis_index("panel")


def high_low(a):
    high = a.astype(jnp.bfloat16)
    return high, (a - high.astype(jnp.float32)).astype(jnp.bfloat16)


def dot3(high, low, v_high, v_low):
    dot = functools.partial(jnp.dot, preferred_element_type=jnp.float32)
    return dot(high, v_high) + (dot(high, v_low) + dot(low, v_high))


def put(v, x, block, columns, value):
    depth = value.shape[0]
    n = v.shape[0] // (3 * depth)
    at = lax.rem(block - x + n, n) * depth
    high, low = high_low(value)
    for part, a in enumerate((high, low, high)):
        v[pl.ds(pl.multiple_of(at + part * n * depth, depth), depth), columns] = a


def put_all(v, x, columns, ref, depth):
    for block in range(ref.shape[0] // depth):
        put(v, x, block, columns, ref[block * depth : (block + 1) * depth, :])


def tile_product(left_refs, v):
    high, low = high_low(jnp.concatenate([ref[...] for ref in left_refs], axis=1))
    return jnp.dot(jnp.concatenate([high, high, low], axis=1), v[...], preferred_element_type=jnp.float32)


def call_kernel(kernel, out_shape, grid, specs, out_specs, scratch, args, flops, traffic):
    return pl.pallas_call(
        kernel,
        out_shape=out_shape,
        grid=(grid,),
        in_specs=specs,
        out_specs=out_specs,
        scratch_shapes=scratch,
        compiler_params=pltpu.CompilerParams(vmem_limit_bytes=67_000_000),
        cost_estimate=pl.CostEstimate(flops=flops, bytes_accessed=traffic, transcendentals=0),
    )(*[pltpu.with_memory_space_constraint(a, pltpu.HBM) for a in args])


def only(on, index):
    return lambda i: jnp.where(place()[1] == on, index(i), 0)


def product_kernel(n_left, picks, width, on, since, *refs):
    n_right = len(picks)
    lefts, rights, (out, held, v, sems) = refs[:n_left], refs[n_left : n_left + n_right], refs[n_left + n_right :]
    i = pl.program_id(0)
    k, core, x = place()

    @pl.when((core == on) & (k >= since))
    def _():
        @pl.when(i == 0)
        def _():
            copies = []
            for j, ref in enumerate(rights):
                source = ref if picks[j] is None else ref.at[picks[j]]
                copies.append(pltpu.make_async_copy(source, held.at[j], sems.at[j]))
                copies[j].start()
            for j, copy in enumerate(copies):
                copy.wait()
                put_all(v, x, slice(j * width, (j + 1) * width), held.at[j], lefts[0].shape[1])

        total = tile_product(lefts, v)
        for j in range(n_right):
            out[j] = total[:, j * width : (j + 1) * width]


def product(left, right, on, since=0):
    rows, depth = left[0][0].shape[-2:]
    width = right[0][0].shape[-1]
    n, full = len(right), len(left) * depth
    step = only(on, lambda i: i)
    return call_kernel(
        functools.partial(product_kernel, len(left), [p[1] for p in right], width, on, since),
        jax.ShapeDtypeStruct((n, rows, width), jnp.float32),
        rows // TILE,
        [spec(p, TILE, step) for p in left] + [pl.BlockSpec(memory_space=pl.ANY)] * n,
        pl.BlockSpec((n, TILE, width), lambda i: (0, step(i), 0)),
        [
            pltpu.VMEM((n, rows, width), jnp.float32),
            pltpu.VMEM((3 * full, n * width), jnp.bfloat16),
            pltpu.SemaphoreType.DMA((n,)),
        ],
        [p[0] for p in left + right],
        6 * rows * full * n * width,
        4 * (rows * full + 2 * n * rows * width),
    )


def chain_kernel(counts, tiles, on, since, passes, *refs):
    n_left = sum(counts)
    lefts, (right, out, v) = refs[:n_left], refs[n_left:]
    i = pl.program_id(0)
    k, core, x = place()
    depth = lefts[0].shape[1]
    blocks = CHAIN_TILE // depth
    tile = lax.rem(i, tiles)
    active = (core == on) & (k >= since)

    @pl.when(active & (i == 0))
    def _():
        put_all(v.at[0], x, slice(None), right, depth)

    at = 0
    for n, count in enumerate(counts):
        here = lefts[at : at + count]
        at += count
        now, later, last = n % 2, (n + 1) % 2, n + 1 == len(counts)
        mine = active & (i >= n * tiles) & (i < (n + 1) * tiles)
        skipped = passes[n] & (k == 0)

        @pl.when(mine & jnp.logical_not(skipped))
        def _(here=here, now=now, later=later, last=last):
            total = tile_product(here, v.at[now])
            if last:
                out[...] = total
            else:
                for h in range(blocks):
                    put(v.at[later], x, tile * blocks + h, slice(None), total[h * depth : (h + 1) * depth])

        @pl.when(mine & skipped)
        def _(now=now, later=later, last=last):
            for h in range(blocks):
                block = lax.rem(tile * blocks + h - x + count, count) * depth
                high = v[now, pl.ds(pl.multiple_of(block, depth), depth), :].astype(jnp.float32)
                low = v[now, pl.ds(pl.multiple_of(block + count * depth, depth), depth), :].astype(jnp.float32)
                if last:
                    out[h * depth : (h + 1) * depth, :] = high + low
                else:
                    put(v.at[later], x, tile * blocks + h, slice(None), high + low)


def chain(lefts, right, on, passes, since=0):
    rows, _ = lefts[0][0][0].shape[-2:]
    width = right[0].shape[-1]
    tiles, n = rows // CHAIN_TILE, len(lefts)
    specs = []
    for m, left in enumerate(lefts):
        specs += [spec(p, CHAIN_TILE, only(on, lambda i, m=m: jnp.clip(i - m * tiles, 0, tiles - 1))) for p in left]
    return call_kernel(
        functools.partial(chain_kernel, [len(left) for left in lefts], tiles, on, since, passes),
        jax.ShapeDtypeStruct((rows, width), jnp.float32),
        n * tiles,
        specs + [spec(right, rows, lambda i: 0)],
        pl.BlockSpec((CHAIN_TILE, width), lambda i: (only(on, lambda i: jnp.maximum(i - (n - 1) * tiles, 0))(i), 0)),
        [pltpu.VMEM((2, 3 * rows, width), jnp.bfloat16)],
        [p[0] for left in lefts for p in left] + [right[0]],
        6 * n * rows * rows * width,
        4 * (n * rows * rows + 2 * rows * width),
    )


def pair_kernel(places, n_x, done, *refs):
    lefts, rights, refs = refs[: len(places)], refs[len(places) : len(places) + 2], refs[len(places) + 2 :]
    i = pl.program_id(0)
    k, core, x = place()
    depth, width, n = lefts[0].shape[1], rights[0].shape[1], len(places)
    v = refs[-1]

    @pl.when(core == 1)
    def _():
        @pl.when(i == 0)
        def _():
            for j, ref in enumerate(rights):
                for at, r in enumerate(places):
                    block = lax.rem(x + r, n_x) * depth
                    high, low = high_low(ref[pl.ds(pl.multiple_of(block, depth), depth), :])
                    for part, a in enumerate((high, low, high)):
                        row = (part * n + at) * depth
                        v[row : row + depth, j * width : (j + 1) * width] = a

        total = tile_product(lefts, v)
        if done:
            begun, passed, step, ahead = refs[:4]
            step[...] = jnp.where(k == 0, passed[...], total[:, :width] + begun[0])
            ahead[...] = total[:, width:] + begun[1]
        else:
            refs[0][0] = total[:, :width]
            refs[0][1] = total[:, width:]


def pair(left, right, begun=None, passed=None):
    first = next(iter(left.values()))
    rows, depth = first[0].shape[-2:]
    width = right[0][0].shape[-1]
    n = len(left)
    both = pl.BlockSpec((2, CHAIN_TILE, width), lambda i: (0, i, 0))
    one = pl.BlockSpec((CHAIN_TILE, width), lambda i: (i, 0))
    f32 = jnp.float32
    specs = [spec(p, CHAIN_TILE, lambda i: i) for p in left.values()] + [spec(p, rows, lambda i: 0) for p in right]
    args = [p[0] for p in [*left.values(), *right]]
    if begun is None:
        out, out_specs = jax.ShapeDtypeStruct((2, rows, width), f32), both
    else:
        out, out_specs = [jax.ShapeDtypeStruct((rows, width), f32)] * 2, [one, one]
        specs += [both, spec(passed, CHAIN_TILE, lambda i: i)]
        args += [begun, passed[0]]
    return call_kernel(
        functools.partial(pair_kernel, tuple(left), rows // depth, begun is not None),
        out,
        rows // CHAIN_TILE,
        specs,
        out_specs,
        [pltpu.VMEM((3 * n * depth, 2 * width), jnp.bfloat16)],
        args,
        12 * rows * n * depth * width,
        4 * (rows * n * depth + 6 * rows * width),
    )


def finish_kernel(scale, late, whole, early, start, token, window, occupancy):
    i = pl.program_id(0)
    k, core, _ = place()

    def write(ref):
        w = ref[...]
        window[...] = w * scale
        part = dot3(*high_low(start[...]), *high_low(w))
        occupancy[...] = jnp.where(i == 0, part, occupancy[...] + part)

    pl.when(core == 1)(functools.partial(write, late))
    pl.when((core == 0) & (k == 0))(functools.partial(write, whole))
    pl.when((core == 0) & (k > 0))(functools.partial(write, early))


def finish(late, whole, early, start, token):
    rows, width = late.shape

    def used(role):
        def index(i):
            k, core, _ = place()
            return jnp.where(jnp.where(core == 1, 0, jnp.where(k == 0, 1, 2)) == role, i, 0)

        return index

    tiles = [spec(p, CHAIN_TILE, used(n)) for n, p in enumerate(((late, None), whole, (early, None)))]
    return call_kernel(
        functools.partial(finish_kernel, float(rows)),
        [jax.ShapeDtypeStruct((rows, width), jnp.float32), jax.ShapeDtypeStruct((1, width), jnp.float32)],
        rows // CHAIN_TILE,
        tiles + [pl.BlockSpec((1, CHAIN_TILE), lambda i: (0, i)), pl.BlockSpec(memory_space=pl.ANY)],
        [pl.BlockSpec((CHAIN_TILE, width), lambda i: (i, 0)), pl.BlockSpec((1, width), lambda i: (0, 0))],
        [],
        [late, whole[0], early, start, token],
        4 * rows * width,
        16 * rows * width,
    )


def body(transitions, start_weights):
    n_tm, n_x = lax.axis_size("tm"), lax.axis_size("panel")
    n_chips = n_tm // 2

    def send(a, even=None, odd=None, wrap=False, since=0):
        pairs = []
        for kk in range(since, n_chips):
            for cc, to in enumerate((even, odd)):
                for xx in range(n_x):
                    if to is not None and (wrap or 0 <= kk + to[0] < n_chips):
                        there = (kk + to[0]) % n_chips * 2 + to[1]
                        pairs.append(((kk * 2 + cc) * n_x + xx, there * n_x + (xx + to[2]) % n_x))
        return lax.ppermute(a, ("tm", "panel"), pairs)

    a, c = transitions[0], lax.optimization_barrier(transitions)[1]
    a_left = send(a, (0, 0, 1), (1, 1, 0), wrap=True)
    c_right = send(c, (0, 0, -1))
    c_left = send(c, (0, 0, 1), (1, 1, 0), wrap=True)
    a_right = send(a, (0, 0, -1))
    a_far = send(a_left, (0, 0, 1))
    c_far = send(c_right, (0, 0, -1))
    token = c_left[:8, :128]
    token = send(token, (0, 1, 0))
    a_odd, c_odd = a_left, c_left
    c_odd_left = send(c_odd, None, (0, 1, 1), since=1)
    a_odd_right = send(a_odd, None, (0, 1, -1))
    c_odd_right = send(c_odd, None, (0, 1, -1), since=1)
    c_odd_far = send(c_odd_left, None, (0, 1, 1), since=1)
    a_odd_far = send(a_odd_right, None, (0, 1, -1))
    a_odd_left = send(a_odd, None, (0, 1, 1))

    def panels(own, right, far, left):
        return [own, (right, None), (far, None), (left, None)]

    def stacked(p):
        return [(p, j) for j in range(n_x)]

    left = panels((transitions, 0), a_right, a_far, a_left)
    right = panels((transitions, 1), c_right, c_far, c_left)
    even = product(left, right, 0)
    even_here = stacked(send(even, (0, 1, 0)))
    even_before = stacked(send(even, (1, 1, 0)))
    left = panels((a_odd, None), a_odd_right, a_odd_far, a_odd_left)
    right = panels((c_odd, None), c_odd_right, c_odd_far, c_odd_left)
    here = even_here[0]
    inner = chain([right], here, 1, (False,), since=1)
    pairs = [(inner, None), right[0]]
    begun = pair({0: left[0], 1: left[1]}, pairs)
    step, ahead = pair({2: left[2], 3: left[3]}, pairs, begun, here)
    there = send(step, None, (-1, 1, 0))
    own = ahead
    ahead = send(ahead, None, (-1, 1, 0), wrap=True)
    rest = product(left, right[1:], 1, since=1)
    odd = [(own, None)] + [(rest, j) for j in range(n_x - 1)]
    step = chain([even_here, odd], (there, None), 1, (False, True))
    early = send(step, None, (1, 0, 0))
    late = chain([even_here, odd, even_before], (ahead, None), 1, (False, True, True))
    window, occupancy = finish(late, (even, 0), early, start_weights[None, :], token)
    return window[None], occupancy


def solution(mesh):
    return jax.shard_map(
        body,
        mesh=mesh,
        in_specs=(P("tm", None, "panel"), P()),
        out_specs=(P("tm", None, "panel"), P("tm", "panel")),
        check_vma=False,
    )
```

```python
import functools

import jax
import jax.numpy as jnp
from jax import lax
from jax.experimental import pallas as pl
from jax.experimental.pallas import tpu as pltpu
from jax.sharding import PartitionSpec as P


TILE = 256
CHAIN_TILE = 512


def spec(panel, rows, index):
    a, j = panel
    if j is None:
        return pl.BlockSpec((rows, a.shape[1]), lambda i: (index(i), 0))
    return pl.BlockSpec((None, rows, a.shape[2]), lambda i: (j, index(i), 0))


def place():
    b = lax.axis_index("tm")
    return b // 2, lax.rem(b, 2), lax.axis_index("panel")


def high_low(a):
    high = a.astype(jnp.bfloat16)
    return high, (a - high.astype(jnp.float32)).astype(jnp.bfloat16)


def dot3(high, low, v_high, v_low):
    dot = functools.partial(jnp.dot, preferred_element_type=jnp.float32)
    return dot(high, v_high) + (dot(high, v_low) + dot(low, v_high))


def put(v, x, block, columns, value):
    depth = value.shape[0]
    n = v.shape[0] // (3 * depth)
    at = lax.rem(block - x + n, n) * depth
    high, low = high_low(value)
    for part, a in enumerate((high, low, high)):
        v[pl.ds(pl.multiple_of(at + part * n * depth, depth), depth), columns] = a


def put_all(v, x, columns, ref, depth):
    for block in range(ref.shape[0] // depth):
        put(v, x, block, columns, ref[block * depth : (block + 1) * depth, :])


def tile_product(left_refs, v):
    high, low = high_low(jnp.concatenate([ref[...] for ref in left_refs], axis=1))
    return jnp.dot(jnp.concatenate([high, high, low], axis=1), v[...], preferred_element_type=jnp.float32)


def call_kernel(kernel, out_shape, grid, specs, out_specs, scratch, args, flops, traffic):
    return pl.pallas_call(
        kernel,
        out_shape=out_shape,
        grid=(grid,),
        in_specs=specs,
        out_specs=out_specs,
        scratch_shapes=scratch,
        compiler_params=pltpu.CompilerParams(vmem_limit_bytes=67_000_000),
        cost_estimate=pl.CostEstimate(flops=flops, bytes_accessed=traffic, transcendentals=0),
    )(*[pltpu.with_memory_space_constraint(a, pltpu.HBM) for a in args])


def only(on, since, index):
    def at(i):
        k, core, _ = place()
        return jnp.where((core == on) & (k >= since), index(i), 0)

    return at


def product_kernel(n_left, picks, width, on, since, *refs):
    n_right = len(picks)
    lefts, rights, (out, held, v, sems) = refs[:n_left], refs[n_left : n_left + n_right], refs[n_left + n_right :]
    i = pl.program_id(0)
    k, core, x = place()

    @pl.when((core == on) & (k >= since))
    def _():
        @pl.when(i == 0)
        def _():
            copies = []
            for j, ref in enumerate(rights):
                source = ref if picks[j] is None else ref.at[picks[j]]
                copies.append(pltpu.make_async_copy(source, held.at[j], sems.at[j]))
                copies[j].start()
            for j, copy in enumerate(copies):
                copy.wait()
                put_all(v, x, slice(j * width, (j + 1) * width), held.at[j], lefts[0].shape[1])

        total = tile_product(lefts, v)
        for j in range(n_right):
            out[j] = total[:, j * width : (j + 1) * width]


def product(left, right, on, since=0):
    rows, depth = left[0][0].shape[-2:]
    width = right[0][0].shape[-1]
    n, full = len(right), len(left) * depth
    step = only(on, since, lambda i: i)
    return call_kernel(
        functools.partial(product_kernel, len(left), [p[1] for p in right], width, on, since),
        jax.ShapeDtypeStruct((n, rows, width), jnp.float32),
        rows // TILE,
        [spec(p, TILE, step) for p in left] + [pl.BlockSpec(memory_space=pl.ANY)] * n,
        pl.BlockSpec((n, TILE, width), lambda i: (0, step(i), 0)),
        [
            pltpu.VMEM((n, rows, width), jnp.float32),
            pltpu.VMEM((3 * full, n * width), jnp.bfloat16),
            pltpu.SemaphoreType.DMA((n,)),
        ],
        [p[0] for p in left + right],
        6 * rows * full * n * width,
        4 * (rows * full + 2 * n * rows * width),
    )


def chain_kernel(counts, tiles, on, since, passes, *refs):
    n_left = sum(counts)
    lefts, (right, out, v) = refs[:n_left], refs[n_left:]
    i = pl.program_id(0)
    k, core, x = place()
    depth = lefts[0].shape[1]
    blocks = CHAIN_TILE // depth
    tile = lax.rem(i, tiles)
    active = (core == on) & (k >= since)

    @pl.when(active & (i == 0))
    def _():
        put_all(v.at[0], x, slice(None), right, depth)

    at = 0
    for n, count in enumerate(counts):
        here = lefts[at : at + count]
        at += count
        now, later, last = n % 2, (n + 1) % 2, n + 1 == len(counts)
        mine = active & (i >= n * tiles) & (i < (n + 1) * tiles)
        skipped = passes[n] & (k == 0)

        @pl.when(mine & jnp.logical_not(skipped))
        def _(here=here, now=now, later=later, last=last):
            total = tile_product(here, v.at[now])
            if last:
                out[...] = total
            else:
                for h in range(blocks):
                    put(v.at[later], x, tile * blocks + h, slice(None), total[h * depth : (h + 1) * depth])

        @pl.when(mine & skipped)
        def _(now=now, later=later, last=last):
            for h in range(blocks):
                block = lax.rem(tile * blocks + h - x + count, count) * depth
                high = v[now, pl.ds(pl.multiple_of(block, depth), depth), :].astype(jnp.float32)
                low = v[now, pl.ds(pl.multiple_of(block + count * depth, depth), depth), :].astype(jnp.float32)
                if last:
                    out[h * depth : (h + 1) * depth, :] = high + low
                else:
                    put(v.at[later], x, tile * blocks + h, slice(None), high + low)


def chain(lefts, right, on, passes, since=0):
    rows, _ = lefts[0][0][0].shape[-2:]
    width = right[0].shape[-1]
    tiles, n = rows // CHAIN_TILE, len(lefts)
    specs = []
    for m, left in enumerate(lefts):
        specs += [spec(p, CHAIN_TILE, only(on, since, lambda i, m=m: jnp.clip(i - m * tiles, 0, tiles - 1))) for p in left]
    return call_kernel(
        functools.partial(chain_kernel, [len(left) for left in lefts], tiles, on, since, passes),
        jax.ShapeDtypeStruct((rows, width), jnp.float32),
        n * tiles,
        specs + [spec(right, rows, lambda i: 0)],
        pl.BlockSpec((CHAIN_TILE, width), lambda i: (only(on, since, lambda i: jnp.maximum(i - (n - 1) * tiles, 0))(i), 0)),
        [pltpu.VMEM((2, 3 * rows, width), jnp.bfloat16)],
        [p[0] for left in lefts for p in left] + [right[0]],
        6 * n * rows * rows * width,
        4 * (n * rows * rows + 2 * rows * width),
    )


def pair_kernel(places, n_x, done, *refs):
    lefts, rights, refs = refs[: len(places)], refs[len(places) : len(places) + 2], refs[len(places) + 2 :]
    i = pl.program_id(0)
    k, core, x = place()
    depth, width, n = lefts[0].shape[1], rights[0].shape[1], len(places)
    v = refs[-1]

    @pl.when(core == 1)
    def _():
        @pl.when(i == 0)
        def _():
            for j, ref in enumerate(rights):
                for at, r in enumerate(places):
                    block = lax.rem(x + r, n_x) * depth
                    high, low = high_low(ref[pl.ds(pl.multiple_of(block, depth), depth), :])
                    for part, a in enumerate((high, low, high)):
                        row = (part * n + at) * depth
                        v[row : row + depth, j * width : (j + 1) * width] = a

        total = tile_product(lefts, v)
        if done:
            begun, passed, step, ahead = refs[:4]
            step[...] = jnp.where(k == 0, passed[...], total[:, :width] + begun[0])
            ahead[...] = total[:, width:] + begun[1]
        else:
            refs[0][0] = total[:, :width]
            refs[0][1] = total[:, width:]


def pair(left, right, begun=None, passed=None):
    first = next(iter(left.values()))
    rows, depth = first[0].shape[-2:]
    width = right[0][0].shape[-1]
    n = len(left)
    both = pl.BlockSpec((2, CHAIN_TILE, width), lambda i: (0, i, 0))
    one = pl.BlockSpec((CHAIN_TILE, width), lambda i: (i, 0))
    f32 = jnp.float32
    specs = [spec(p, CHAIN_TILE, lambda i: i) for p in left.values()] + [spec(p, rows, lambda i: 0) for p in right]
    args = [p[0] for p in [*left.values(), *right]]
    if begun is None:
        out, out_specs = jax.ShapeDtypeStruct((2, rows, width), f32), both
    else:
        out, out_specs = [jax.ShapeDtypeStruct((rows, width), f32)] * 2, [one, one]
        specs += [both, spec(passed, CHAIN_TILE, lambda i: i)]
        args += [begun, passed[0]]
    return call_kernel(
        functools.partial(pair_kernel, tuple(left), rows // depth, begun is not None),
        out,
        rows // CHAIN_TILE,
        specs,
        out_specs,
        [pltpu.VMEM((3 * n * depth, 2 * width), jnp.bfloat16)],
        args,
        12 * rows * n * depth * width,
        4 * (rows * n * depth + 6 * rows * width),
    )


def finish_kernel(scale, late, whole, early, start, token, window, occupancy):
    i = pl.program_id(0)
    k, core, _ = place()

    def write(ref):
        w = ref[...]
        window[...] = w * scale
        part = dot3(*high_low(start[...]), *high_low(w))
        occupancy[...] = jnp.where(i == 0, part, occupancy[...] + part)

    pl.when(core == 1)(functools.partial(write, late))
    pl.when((core == 0) & (k == 0))(functools.partial(write, whole))
    pl.when((core == 0) & (k > 0))(functools.partial(write, early))


def finish(late, whole, early, start, token):
    rows, width = late.shape

    def used(role):
        def index(i):
            k, core, _ = place()
            return jnp.where(jnp.where(core == 1, 0, jnp.where(k == 0, 1, 2)) == role, i, 0)

        return index

    tiles = [spec(p, CHAIN_TILE, used(n)) for n, p in enumerate(((late, None), whole, (early, None)))]
    return call_kernel(
        functools.partial(finish_kernel, float(rows)),
        [jax.ShapeDtypeStruct((rows, width), jnp.float32), jax.ShapeDtypeStruct((1, width), jnp.float32)],
        rows // CHAIN_TILE,
        tiles + [pl.BlockSpec((1, CHAIN_TILE), lambda i: (0, i)), pl.BlockSpec(memory_space=pl.ANY)],
        [pl.BlockSpec((CHAIN_TILE, width), lambda i: (i, 0)), pl.BlockSpec((1, width), lambda i: (0, 0))],
        [],
        [late, whole[0], early, start, token],
        4 * rows * width,
        16 * rows * width,
    )


def body(transitions, start_weights):
    n_tm, n_x = lax.axis_size("tm"), lax.axis_size("panel")
    n_chips = n_tm // 2

    def send(a, even=None, odd=None, wrap=False, since=0):
        pairs = []
        for kk in range(since, n_chips):
            for cc, to in enumerate((even, odd)):
                for xx in range(n_x):
                    if to is not None and (wrap or 0 <= kk + to[0] < n_chips):
                        there = (kk + to[0]) % n_chips * 2 + to[1]
                        pairs.append(((kk * 2 + cc) * n_x + xx, there * n_x + (xx + to[2]) % n_x))
        return lax.ppermute(a, ("tm", "panel"), pairs)

    a, c = transitions[0], lax.optimization_barrier(transitions)[1]
    a_left = send(a, (0, 0, 1), (1, 1, 0), wrap=True)
    c_right = send(c, (0, 0, -1))
    c_left = send(c, (0, 0, 1), (1, 1, 0), wrap=True)
    a_right = send(a, (0, 0, -1))
    a_far = send(a_left, (0, 0, 1))
    c_far = send(c_right, (0, 0, -1))
    token = c_left[:8, :128]
    token = send(token, (0, 1, 0))
    a_odd, c_odd = a_left, c_left
    c_odd_left = send(c_odd, None, (0, 1, 1), since=1)
    a_odd_right = send(a_odd, None, (0, 1, -1))
    c_odd_right = send(c_odd, None, (0, 1, -1), since=1)
    c_odd_far = send(c_odd_left, None, (0, 1, 1), since=1)
    a_odd_far = send(a_odd_right, None, (0, 1, -1))
    a_odd_left = send(a_odd, None, (0, 1, 1))

    def panels(own, right, far, left):
        return [own, (right, None), (far, None), (left, None)]

    def stacked(p):
        return [(p, j) for j in range(n_x)]

    left = panels((transitions, 0), a_right, a_far, a_left)
    right = panels((transitions, 1), c_right, c_far, c_left)
    even = product(left, right, 0)
    even_here = stacked(send(even, (0, 1, 0)))
    even_before = stacked(send(even, (1, 1, 0)))
    left = panels((a_odd, None), a_odd_right, a_odd_far, a_odd_left)
    right = panels((c_odd, None), c_odd_right, c_odd_far, c_odd_left)
    here = even_here[0]
    inner = chain([right], here, 1, (False,), since=1)
    pairs = [(inner, None), right[0]]
    begun = pair({0: left[0], 1: left[1]}, pairs)
    step, ahead = pair({2: left[2], 3: left[3]}, pairs, begun, here)
    there = send(step, None, (-1, 1, 0))
    own = ahead
    ahead = send(ahead, None, (-1, 1, 0), wrap=True)
    rest = product(left, right[1:], 1, since=1)
    odd = [(own, None)] + [(rest, j) for j in range(n_x - 1)]
    step = chain([even_here, odd], (there, None), 1, (False, True))
    early = send(step, None, (1, 0, 0))
    late = chain([even_here, odd, even_before], (ahead, None), 1, (False, True, True))
    window, occupancy = finish(late, (even, 0), early, start_weights[None, :], token)
    return window[None], occupancy


def solution(mesh):
    return jax.shard_map(
        body,
        mesh=mesh,
        in_specs=(P("tm", None, "panel"), P()),
        out_specs=(P("tm", None, "panel"), P("tm", "panel")),
        check_vma=False,
    )
```

```python
import functools

import jax
import jax.numpy as jnp
from jax import lax
from jax.experimental import pallas as pl
from jax.experimental.pallas import tpu as pltpu
from jax.sharding import PartitionSpec as P


TILE = 256
CHAIN_TILE = 512


def spec(panel, rows, index):
    a, j = panel
    if j is None:
        return pl.BlockSpec((rows, a.shape[1]), lambda i: (index(i), 0))
    return pl.BlockSpec((None, rows, a.shape[2]), lambda i: (j, index(i), 0))


def place():
    b = lax.axis_index("tm")
    return b // 2, lax.rem(b, 2), lax.axis_index("panel")


def high_low(a):
    high = a.astype(jnp.bfloat16)
    return high, (a - high.astype(jnp.float32)).astype(jnp.bfloat16)


def dot3(high, low, v_high, v_low):
    dot = functools.partial(jnp.dot, preferred_element_type=jnp.float32)
    return dot(high, v_high) + (dot(high, v_low) + dot(low, v_high))


def put(v, x, block, columns, value):
    depth = value.shape[0]
    n = v.shape[0] // (3 * depth)
    at = lax.rem(block - x + n, n) * depth
    high, low = high_low(value)
    for part, a in enumerate((high, low, high)):
        v[pl.ds(pl.multiple_of(at + part * n * depth, depth), depth), columns] = a


def put_all(v, x, columns, ref, depth):
    for block in range(ref.shape[0] // depth):
        put(v, x, block, columns, ref[block * depth : (block + 1) * depth, :])


def tile_product(left_refs, v):
    high, low = high_low(jnp.concatenate([ref[...] for ref in left_refs], axis=1))
    return jnp.dot(jnp.concatenate([high, high, low], axis=1), v[...], preferred_element_type=jnp.float32)


def call_kernel(kernel, out_shape, grid, specs, out_specs, scratch, args, flops, traffic):
    return pl.pallas_call(
        kernel,
        out_shape=out_shape,
        grid=(grid,),
        in_specs=specs,
        out_specs=out_specs,
        scratch_shapes=scratch,
        compiler_params=pltpu.CompilerParams(vmem_limit_bytes=67_000_000),
        cost_estimate=pl.CostEstimate(flops=flops, bytes_accessed=traffic, transcendentals=0),
    )(*[pltpu.with_memory_space_constraint(a, pltpu.HBM) for a in args])


def only(on, since, index):
    def at(i):
        k, core, _ = place()
        return jnp.where((core == on) & (k >= since), index(i), 0)

    return at


def product_kernel(n_left, picks, width, on, since, *refs):
    n_right = len(picks)
    lefts, rights, (out, held, v, sems) = refs[:n_left], refs[n_left : n_left + n_right], refs[n_left + n_right :]
    i = pl.program_id(0)
    k, core, x = place()

    @pl.when((core == on) & (k >= since))
    def _():
        @pl.when(i == 0)
        def _():
            copies = []
            for j, ref in enumerate(rights):
                source = ref if picks[j] is None else ref.at[picks[j]]
                copies.append(pltpu.make_async_copy(source, held.at[j], sems.at[j]))
                copies[j].start()
            for j, copy in enumerate(copies):
                copy.wait()
                put_all(v, x, slice(j * width, (j + 1) * width), held.at[j], lefts[0].shape[1])

        total = tile_product(lefts, v)
        for j in range(n_right):
            out[j] = total[:, j * width : (j + 1) * width]


def product(left, right, on, since=0, tile=TILE):
    rows, depth = left[0][0].shape[-2:]
    width = right[0][0].shape[-1]
    n, full = len(right), len(left) * depth
    step = only(on, since, lambda i: i)
    return call_kernel(
        functools.partial(product_kernel, len(left), [p[1] for p in right], width, on, since),
        jax.ShapeDtypeStruct((n, rows, width), jnp.float32),
        rows // tile,
        [spec(p, tile, step) for p in left] + [pl.BlockSpec(memory_space=pl.ANY)] * n,
        pl.BlockSpec((n, tile, width), lambda i: (0, step(i), 0)),
        [
            pltpu.VMEM((n, rows, width), jnp.float32),
            pltpu.VMEM((3 * full, n * width), jnp.bfloat16),
            pltpu.SemaphoreType.DMA((n,)),
        ],
        [p[0] for p in left + right],
        6 * rows * full * n * width,
        4 * (rows * full + 2 * n * rows * width),
    )


def chain_kernel(counts, tiles, on, since, passes, *refs):
    n_left = sum(counts)
    lefts, (right, out, v) = refs[:n_left], refs[n_left:]
    i = pl.program_id(0)
    k, core, x = place()
    depth = lefts[0].shape[1]
    blocks = CHAIN_TILE // depth
    tile = lax.rem(i, tiles)
    active = (core == on) & (k >= since)

    @pl.when(active & (i == 0))
    def _():
        put_all(v.at[0], x, slice(None), right, depth)

    at = 0
    for n, count in enumerate(counts):
        here = lefts[at : at + count]
        at += count
        now, later, last = n % 2, (n + 1) % 2, n + 1 == len(counts)
        mine = active & (i >= n * tiles) & (i < (n + 1) * tiles)
        skipped = passes[n] & (k == 0)

        @pl.when(mine & jnp.logical_not(skipped))
        def _(here=here, now=now, later=later, last=last):
            total = tile_product(here, v.at[now])
            if last:
                out[...] = total
            else:
                for h in range(blocks):
                    put(v.at[later], x, tile * blocks + h, slice(None), total[h * depth : (h + 1) * depth])

        @pl.when(mine & skipped)
        def _(now=now, later=later, last=last):
            for h in range(blocks):
                block = lax.rem(tile * blocks + h - x + count, count) * depth
                high = v[now, pl.ds(pl.multiple_of(block, depth), depth), :].astype(jnp.float32)
                low = v[now, pl.ds(pl.multiple_of(block + count * depth, depth), depth), :].astype(jnp.float32)
                if last:
                    out[h * depth : (h + 1) * depth, :] = high + low
                else:
                    put(v.at[later], x, tile * blocks + h, slice(None), high + low)


def chain(lefts, right, on, passes, since=0):
    rows, _ = lefts[0][0][0].shape[-2:]
    width = right[0].shape[-1]
    tiles, n = rows // CHAIN_TILE, len(lefts)
    specs = []
    for m, left in enumerate(lefts):
        specs += [spec(p, CHAIN_TILE, only(on, since, lambda i, m=m: jnp.clip(i - m * tiles, 0, tiles - 1))) for p in left]
    return call_kernel(
        functools.partial(chain_kernel, [len(left) for left in lefts], tiles, on, since, passes),
        jax.ShapeDtypeStruct((rows, width), jnp.float32),
        n * tiles,
        specs + [spec(right, rows, lambda i: 0)],
        pl.BlockSpec((CHAIN_TILE, width), lambda i: (only(on, since, lambda i: jnp.maximum(i - (n - 1) * tiles, 0))(i), 0)),
        [pltpu.VMEM((2, 3 * rows, width), jnp.bfloat16)],
        [p[0] for left in lefts for p in left] + [right[0]],
        6 * n * rows * rows * width,
        4 * (n * rows * rows + 2 * rows * width),
    )


def pair_kernel(places, n_x, done, *refs):
    lefts, rights, refs = refs[: len(places)], refs[len(places) : len(places) + 2], refs[len(places) + 2 :]
    i = pl.program_id(0)
    k, core, x = place()
    depth, width, n = lefts[0].shape[1], rights[0].shape[1], len(places)
    v = refs[-1]

    @pl.when(core == 1)
    def _():
        @pl.when(i == 0)
        def _():
            for j, ref in enumerate(rights):
                for at, r in enumerate(places):
                    block = lax.rem(x + r, n_x) * depth
                    high, low = high_low(ref[pl.ds(pl.multiple_of(block, depth), depth), :])
                    for part, a in enumerate((high, low, high)):
                        row = (part * n + at) * depth
                        v[row : row + depth, j * width : (j + 1) * width] = a

        total = tile_product(lefts, v)
        if done:
            begun, passed, step, ahead = refs[:4]
            step[...] = jnp.where(k == 0, passed[...], total[:, :width] + begun[0])
            ahead[...] = total[:, width:] + begun[1]
        else:
            refs[0][0] = total[:, :width]
            refs[0][1] = total[:, width:]


def pair(left, right, begun=None, passed=None):
    first = next(iter(left.values()))
    rows, depth = first[0].shape[-2:]
    width = right[0][0].shape[-1]
    n = len(left)
    both = pl.BlockSpec((2, CHAIN_TILE, width), lambda i: (0, i, 0))
    one = pl.BlockSpec((CHAIN_TILE, width), lambda i: (i, 0))
    f32 = jnp.float32
    specs = [spec(p, CHAIN_TILE, lambda i: i) for p in left.values()] + [spec(p, rows, lambda i: 0) for p in right]
    args = [p[0] for p in [*left.values(), *right]]
    if begun is None:
        out, out_specs = jax.ShapeDtypeStruct((2, rows, width), f32), both
    else:
        out, out_specs = [jax.ShapeDtypeStruct((rows, width), f32)] * 2, [one, one]
        specs += [both, spec(passed, CHAIN_TILE, lambda i: i)]
        args += [begun, passed[0]]
    return call_kernel(
        functools.partial(pair_kernel, tuple(left), rows // depth, begun is not None),
        out,
        rows // CHAIN_TILE,
        specs,
        out_specs,
        [pltpu.VMEM((3 * n * depth, 2 * width), jnp.bfloat16)],
        args,
        12 * rows * n * depth * width,
        4 * (rows * n * depth + 6 * rows * width),
    )


def finish_kernel(scale, late, whole, early, start, token, window, occupancy):
    i = pl.program_id(0)
    k, core, _ = place()

    def write(ref):
        w = ref[...]
        window[...] = w * scale
        part = dot3(*high_low(start[...]), *high_low(w))
        occupancy[...] = jnp.where(i == 0, part, occupancy[...] + part)

    pl.when(core == 1)(functools.partial(write, late))
    pl.when((core == 0) & (k == 0))(functools.partial(write, whole))
    pl.when((core == 0) & (k > 0))(functools.partial(write, early))


def finish(late, whole, early, start, token):
    rows, width = late.shape

    def used(role):
        def index(i):
            k, core, _ = place()
            return jnp.where(jnp.where(core == 1, 0, jnp.where(k == 0, 1, 2)) == role, i, 0)

        return index

    tiles = [spec(p, CHAIN_TILE, used(n)) for n, p in enumerate(((late, None), whole, (early, None)))]
    return call_kernel(
        functools.partial(finish_kernel, float(rows)),
        [jax.ShapeDtypeStruct((rows, width), jnp.float32), jax.ShapeDtypeStruct((1, width), jnp.float32)],
        rows // CHAIN_TILE,
        tiles + [pl.BlockSpec((1, CHAIN_TILE), lambda i: (0, i)), pl.BlockSpec(memory_space=pl.ANY)],
        [pl.BlockSpec((CHAIN_TILE, width), lambda i: (i, 0)), pl.BlockSpec((1, width), lambda i: (0, 0))],
        [],
        [late, whole[0], early, start, token],
        4 * rows * width,
        16 * rows * width,
    )


def body(transitions, start_weights):
    n_tm, n_x = lax.axis_size("tm"), lax.axis_size("panel")
    n_chips = n_tm // 2

    def send(a, even=None, odd=None, wrap=False, since=0):
        pairs = []
        for kk in range(since, n_chips):
            for cc, to in enumerate((even, odd)):
                for xx in range(n_x):
                    if to is not None and (wrap or 0 <= kk + to[0] < n_chips):
                        there = (kk + to[0]) % n_chips * 2 + to[1]
                        pairs.append(((kk * 2 + cc) * n_x + xx, there * n_x + (xx + to[2]) % n_x))
        return lax.ppermute(a, ("tm", "panel"), pairs)

    a, c = transitions[0], lax.optimization_barrier(transitions)[1]
    a_left = send(a, (0, 0, 1), (1, 1, 0), wrap=True)
    c_right = send(c, (0, 0, -1))
    c_left = send(c, (0, 0, 1), (1, 1, 0), wrap=True)
    a_right = send(a, (0, 0, -1))
    a_far = send(a_left, (0, 0, 1))
    c_far = send(c_right, (0, 0, -1))
    token = c_left[:8, :128]
    token = send(token, (0, 1, 0))
    a_odd, c_odd = a_left, c_left
    c_odd_left = send(c_odd, None, (0, 1, 1), since=1)
    a_odd_right = send(a_odd, None, (0, 1, -1))
    c_odd_right = send(c_odd, None, (0, 1, -1), since=1)
    c_odd_far = send(c_odd_left, None, (0, 1, 1), since=1)
    a_odd_far = send(a_odd_right, None, (0, 1, -1))
    a_odd_left = send(a_odd, None, (0, 1, 1))

    def panels(own, right, far, left):
        return [own, (right, None), (far, None), (left, None)]

    def stacked(p):
        return [(p, j) for j in range(n_x)]

    left = panels((transitions, 0), a_right, a_far, a_left)
    right = panels((transitions, 1), c_right, c_far, c_left)
    even = product(left, right, 0)
    even_here = stacked(send(even, (0, 1, 0)))
    even_before = stacked(send(even, (1, 1, 0)))
    left = panels((a_odd, None), a_odd_right, a_odd_far, a_odd_left)
    right = panels((c_odd, None), c_odd_right, c_odd_far, c_odd_left)
    here = even_here[0]
    inner = chain([right], here, 1, (False,), since=1)
    pairs = [(inner, None), right[0]]
    begun = pair({0: left[0], 1: left[1]}, pairs)
    step, ahead = pair({2: left[2], 3: left[3]}, pairs, begun, here)
    there = send(step, None, (-1, 1, 0))
    own = ahead
    ahead = send(ahead, None, (-1, 1, 0), wrap=True)
    rest = product(left, right[1:], 1, since=1, tile=CHAIN_TILE)
    odd = [(own, None)] + [(rest, j) for j in range(n_x - 1)]
    step = chain([even_here, odd], (there, None), 1, (False, True))
    early = send(step, None, (1, 0, 0))
    late = chain([even_here, odd, even_before], (ahead, None), 1, (False, True, True))
    window, occupancy = finish(late, (even, 0), early, start_weights[None, :], token)
    return window[None], occupancy


def solution(mesh):
    return jax.shard_map(
        body,
        mesh=mesh,
        in_specs=(P("tm", None, "panel"), P()),
        out_specs=(P("tm", None, "panel"), P("tm", "panel")),
        check_vma=False,
    )
```
